32 devices in a mesh: row: 8 (over z, y), col: 4 (over x, core).
Axes of the slice: x: 2, y: 2, z: 4, core: 2. Of those that a mesh axis runs over, the one named last changes fastest.
Arguments:
- orbitals: bfloat16 [20480, 384], P(('row', 'col')), may hold values from -6 to 6
- coulomb: float32 [20480, 20480], P('row', 'col'), may hold values from -0.001953125 to 0.001953125
- interp: bfloat16 [4096, 20480], P('row', 'col'), may hold values from -0.0390625 to 0.0390625
Outputs:
- exchanged: bfloat16 [4096, 384], P(('row', 'col'))
The draws below stay inside these ranges and needn't reach their ends.
All inputs are finite; a program needn't handle non-finite values.
Results may differ from the reference program's by a relative error of at most 0.018.
Values may be sent and summed in bfloat16 or wider, within the bound.
No kernel may reach another device: no remote copies, remote signals or barrier semaphores. Data moves between devices by JAX's collectives and lax.ppermute only.
A program may use at most 128 MiB of HBM per device.

```python
import math
import jax
import jax.numpy as jnp
from jax import lax

NMU = 20480
NORB = 384
GRID = 4096


def block_scale(rng, dims, cuts, low, top_value):
    factor_of, own = 1.0, jax.random.fold_in(rng, 6)
    for position, parts in cuts:
        steps = jnp.exp(jax.random.uniform(jax.random.fold_in(own, position), (parts,), jnp.float32, low / len(cuts), top_value / len(cuts)))
        factor_of = factor_of * jnp.repeat(steps, dims[position] // parts).reshape([-1 if axis == position else 1 for axis in range(len(dims))])
    return factor_of


def noise(own_key, shape, deviation, bound, split=(), kind=jnp.bfloat16):
    drawn = jax.random.normal(own_key, shape, jnp.float32) * deviation
    if len(split) > 0:
        drawn = block_scale(own_key, shape, split, -0.22, 0.18) * drawn
    return jnp.clip(drawn, min=-bound, max=bound).astype(kind)


def setup_inputs(seed: int = 0) -> dict:
    streams_of = jax.random.split(jax.random.key(seed), 4)
    return {
        "orbitals": noise(streams_of[0], (NMU, NORB), 1.0, 6.0, ((0, 32),)),
        "coulomb": noise(streams_of[1], (NMU, NMU), (1.0 / (NORB * NMU) ** 0.5), 0.001953125, ((0, 8), (1, 4)), jnp.float32),
        "interp": noise(streams_of[2], (GRID, NMU), NMU ** -0.5, 0.0390625, ((0, 8), (1, 4))),
    }


def reference(orbitals, coulomb, interp):
    block = math.gcd(NMU, 512)

    def step(total, index):
        start = (index * block).astype(jnp.int32)
        rows = lax.dynamic_slice_in_dim(orbitals, start, block, 0)
        kernel = lax.dynamic_slice_in_dim(coulomb, start, block, 0)
        density = jnp.dot(rows, orbitals.T, preferred_element_type=jnp.float32)
        weighted = (kernel * density).astype(jnp.bfloat16)
        return total + jnp.dot(weighted.T, rows, preferred_element_type=jnp.float32), None

    total, unused = lax.scan(step, jnp.zeros((NMU, NORB), jnp.float32), jnp.arange(NMU // block, dtype=jnp.int32))
    contracted = total.astype(jnp.bfloat16)
    return jnp.dot(interp, contracted, preferred_element_type=jnp.float32).astype(jnp.bfloat16)
```

```python
import functools

import jax
import jax.numpy as jnp
from jax import lax
from jax.experimental import pallas as pl
from jax.experimental.pallas import tpu as pltpu
from jax.sharding import PartitionSpec as P

AXES = ("row", "col")


def plan(rows, cols):
    factor = rows // cols
    half = cols // 2

    def turn(c):
        return c if cols == 1 else (c >> 1) | ((c & 1) * half)

    ring = []
    for y in range(factor):
        zs = range(cols) if y % 2 == 0 else reversed(range(cols))
        ring += [z * factor + y for z in zs]
    position = {row: p for p, row in enumerate(ring)}
    back = {turn(c): c for c in range(cols)}
    piece = [(row % factor) * cols + back[row // factor] for row in ring]

    deal = []
    for row in range(rows):
        z, y = divmod(row, factor)
        for c in range(cols):
            deal.append((row * cols + c, (turn(c) * factor + y) * cols + z))
    hop = []
    table = []
    for row in range(rows):
        p = position[row]
        table.append([])
        for c in range(cols):
            step = 1 if c % 2 == 0 else -1
            hop.append((row * cols + c, ring[(p + step) % rows] * cols + c))
            table[-1].append([piece[(p - step * k) % rows] for k in range(rows)])

    def swap(bit):
        return [(r * cols + c, r * cols + (c ^ bit)) for r in range(rows) for c in range(cols)]

    return deal, hop, swap, table


def divisor(total, target, unit):
    best = unit
    for size in range(unit, min(total, target) + 1, unit):
        if total % size == 0:
            best = size
    return best


def partial_kernel(where, near_ref, turned_ref, far_ref, coulomb_ref, out_ref):
    @pl.when(pl.program_id(0) == 0)
    def _():
        out_ref[...] = jnp.zeros_like(out_ref)

    density = lax.dot_general(
        near_ref[...], far_ref[...], (((1,), (1,)), ((), ())), preferred_element_type=jnp.float32
    )
    weighted = (coulomb_ref[...] * density).astype(jnp.bfloat16)
    out_ref[...] += jnp.dot(turned_ref[...], weighted, preferred_element_type=jnp.float32)


def partial_of(where, near, turned, far, coulomb):
    m, norb = near.shape
    width = far.shape[0]
    tile = divisor(m, 640, 128)
    if width % 128 or m % tile:
        block = lax.dynamic_slice_in_dim(coulomb, where[0] * width, width, 1)
        density = jnp.dot(near, far.T, preferred_element_type=jnp.float32)
        weighted = (block * density).astype(jnp.bfloat16)
        return jnp.dot(turned, weighted, preferred_element_type=jnp.float32)
    return pl.pallas_call(
        partial_kernel,
        out_shape=jax.ShapeDtypeStruct((norb, width), jnp.float32),
        grid_spec=pltpu.PrefetchScalarGridSpec(
            num_scalar_prefetch=1,
            grid=(m // tile,),
            in_specs=[
                pl.BlockSpec((tile, norb), lambda i, w: (i, 0)),
                pl.BlockSpec((norb, tile), lambda i, w: (0, i)),
                pl.BlockSpec((width, norb), lambda i, w: (0, 0)),
                pl.BlockSpec((tile, width), lambda i, w: (i, w[0])),
            ],
            out_specs=pl.BlockSpec((norb, width), lambda i, w: (0, 0)),
        ),
        compiler_params=pltpu.CompilerParams(vmem_limit_bytes=48 << 20),
        cost_estimate=pl.CostEstimate(
            flops=4 * m * norb * width, bytes_accessed=4 * m * width + 8 * m * norb, transcendentals=0
        ),
        name="partial",
    )(where, near, turned, far, coulomb)


def term_kernel(where, interp_ref, piece_ref, total_ref, out_ref):
    out_ref[...] = total_ref[...] + lax.dot_general(
        interp_ref[...], piece_ref[...], (((1,), (1,)), ((), ())), preferred_element_type=jnp.float32
    )


def term_of(where, interp, piece, total):
    g = interp.shape[0]
    norb, width = piece.shape
    if width % 128:
        block = lax.dynamic_slice_in_dim(interp, where[0] * width, width, 1)
        return total + jnp.dot(block, piece.T, preferred_element_type=jnp.float32)
    whole = pl.BlockSpec((g, norb), lambda i, w: (0, 0))
    return pl.pallas_call(
        term_kernel,
        out_shape=jax.ShapeDtypeStruct((g, norb), jnp.float32),
        grid_spec=pltpu.PrefetchScalarGridSpec(
            num_scalar_prefetch=1,
            grid=(1,),
            in_specs=[
                pl.BlockSpec((g, width), lambda i, w: (0, w[0])),
                pl.BlockSpec((norb, width), lambda i, w: (0, 0)),
                whole,
            ],
            out_specs=whole,
        ),
        compiler_params=pltpu.CompilerParams(vmem_limit_bytes=32 << 20),
        cost_estimate=pl.CostEstimate(
            flops=2 * g * norb * width,
            bytes_accessed=2 * (g + norb) * width + 8 * g * norb,
            transcendentals=0,
        ),
        name="term",
    )(where, interp, piece, total)


def local(rows, cols, orbitals, coulomb, interp):
    deal, hop, swap, table = plan(rows, cols)
    share, norb = orbitals.shape
    row, col = lax.axis_index("row"), lax.axis_index("col")
    where = lax.dynamic_slice(
        jnp.asarray(table, jnp.int32), (row, col, 0), (1, 1, rows)
    ).reshape(rows)

    far = lax.ppermute(orbitals, AXES, deal)
    held = [(0, orbitals)]
    bit = cols // 2
    while bit:
        held += [(mask ^ bit, lax.ppermute(block, AXES, swap(bit))) for mask, block in held]
        bit //= 2
    near = jnp.zeros((cols * share, norb), orbitals.dtype)
    for mask, block in held:
        near = lax.dynamic_update_slice(near, block, ((col ^ mask) * share, 0))
    turned = near.T

    sent = None
    for k in range(rows):
        following = lax.ppermute(far, AXES, hop) if k < rows - 1 else None
        part = partial_of(where[k : k + 1], near, turned, far, coulomb)
        if sent is not None:
            part = part + lax.ppermute(sent, AXES, hop).astype(jnp.float32)
        sent = part.astype(jnp.bfloat16)
        far = following

    piece = sent
    total = jnp.zeros((interp.shape[0], norb), jnp.float32)
    for k in range(rows):
        following = lax.ppermute(piece, AXES, hop) if k < rows - 1 else None
        at = (k - 1) % rows
        total = term_of(where[at : at + 1], interp, piece, total)
        piece = following

    bit, blocks = 1, cols
    while bit < cols:
        pairs = total.reshape(blocks // 2, 2, -1, norb)
        mine = (col // bit) % 2
        keep = lax.dynamic_index_in_dim(pairs, mine, 1, keepdims=False)
        give = lax.dynamic_index_in_dim(pairs, 1 - mine, 1, keepdims=False)
        total = keep + lax.ppermute(give.astype(jnp.bfloat16), AXES, swap(bit)).astype(jnp.float32)
        bit, blocks = bit * 2, blocks // 2
    return total.reshape(-1, norb).astype(jnp.bfloat16)


def solution(mesh):
    in_specs = (P(("row", "col"), None), P("row", "col"), P("row", "col"))
    out_specs = P(("row", "col"), None)
    body = functools.partial(local, mesh.shape["row"], mesh.shape["col"])
    return jax.shard_map(body, mesh=mesh, in_specs=in_specs, out_specs=out_specs, check_vma=False)
```

```python
import functools

import jax
import jax.numpy as jnp
from jax import lax
from jax.experimental import pallas as pl
from jax.experimental.pallas import tpu as pltpu
from jax.sharding import PartitionSpec as P

AXES = ("row", "col")
NT = (((1,), (1,)), ((), ()))
TN = (((0,), (0,)), ((), ()))


def plan(rows, cols):
    factor = rows // cols
    half = max(cols // 2, 1)

    def turn(c, target):
        return (c & 1) * half | ((c >> 1) ^ (target & (1 if half > 1 else 0)))

    ring = []
    for y in range(factor):
        zs = range(cols) if y % 2 == 0 else reversed(range(cols))
        ring += [z * factor + y for z in zs]
    position = {row: p for p, row in enumerate(ring)}

    deal, hop, table = [], [], []
    for row in range(rows):
        z, y = divmod(row, factor)
        for c in range(cols):
            deal.append((row * cols + c, (turn(c, z) * factor + y) * cols + z))
    for row in range(rows):
        p = position[row]
        table.append([])
        for c in range(cols):
            back = {turn(s, c): s for s in range(cols)}
            piece = [(r % factor) * cols + back[r // factor] for r in ring]
            step = 1 if c % 2 == 0 else -1
            hop.append((row * cols + c, ring[(p + step) % rows] * cols + c))
            passing = [piece[(p - step * k) % rows] for k in range(rows)]
            table[-1].append(passing + [c ^ mask for mask in range(cols)])

    def swap(bit):
        return [(r * cols + c, r * cols + (c ^ bit)) for r in range(rows) for c in range(cols)]

    return deal, hop, swap, table


def accumulate(near, far_ref, coulomb_ref, out_ref):
    @pl.when(pl.program_id(0) == 0)
    def _():
        out_ref[...] = jnp.zeros_like(out_ref)

    density = lax.dot_general(near, far_ref[...], NT, preferred_element_type=jnp.float32)
    weighted = (coulomb_ref[...] * density).astype(jnp.bfloat16)
    out_ref[...] += lax.dot_general(near, weighted, TN, preferred_element_type=jnp.float32)


def first_kernel(count, where, *refs):
    shards, (far_ref, coulomb_ref, out_ref, near_ref) = refs[:count], refs[count:]
    share = shards[0].shape[0]
    for q in range(count):

        @pl.when(pl.program_id(0) == q)
        def _():
            near_ref[q * share : (q + 1) * share, :] = shards[q][...]

    rows = pl.ds(pl.multiple_of(pl.program_id(0) * share, share), share)
    accumulate(near_ref[rows, :], far_ref, coulomb_ref, out_ref)


def next_kernel(where, near_ref, far_ref, coulomb_ref, out_ref):
    accumulate(near_ref[...], far_ref, coulomb_ref, out_ref)


def partial_of(k, where, near, far, coulomb):
    first = isinstance(near, list)
    count = len(near) if first else near.shape[0] // far.shape[0]
    share, norb = far.shape
    rows = where.shape[0] - count
    if share % 128:
        if first:
            near = jnp.concatenate(near, 0)
        column = lax.dynamic_slice_in_dim(coulomb, where[k] * share, share, 1)
        column = jnp.take(column.reshape(count, share, share), where[rows:], axis=0)
        density = lax.dot_general(near, far, NT, preferred_element_type=jnp.float32)
        weighted = (column.reshape(-1, share) * density).astype(jnp.bfloat16)
        return lax.dot_general(near, weighted, TN, preferred_element_type=jnp.float32), near

    fixed = lambda i, w: (0, 0)
    sums = jax.ShapeDtypeStruct((norb, share), jnp.float32)
    sums_spec = pl.BlockSpec((norb, share), fixed)
    shard_spec = pl.BlockSpec((share, norb), fixed)
    tail_specs = [shard_spec, pl.BlockSpec((share, share), lambda i, w: (w[rows + i], w[k]))]
    m = count * share
    options = dict(
        compiler_params=pltpu.CompilerParams(vmem_limit_bytes=20 << 20),
        cost_estimate=pl.CostEstimate(
            flops=4 * m * norb * share, bytes_accessed=4 * m * share, transcendentals=0
        ),
        name="partial",
    )
    if first:
        return pl.pallas_call(
            functools.partial(first_kernel, count),
            out_shape=(sums, jax.ShapeDtypeStruct((m, norb), jnp.bfloat16)),
            grid_spec=pltpu.PrefetchScalarGridSpec(
                num_scalar_prefetch=1,
                grid=(count,),
                in_specs=[shard_spec] * count + tail_specs,
                out_specs=(sums_spec, pl.BlockSpec((m, norb), fixed)),
            ),
            **options,
        )(where, *near, far, coulomb)
    return pl.pallas_call(
        next_kernel,
        out_shape=sums,
        grid_spec=pltpu.PrefetchScalarGridSpec(
            num_scalar_prefetch=1,
            grid=(count,),
            in_specs=[pl.BlockSpec((share, norb), lambda i, w: (i, 0))] + tail_specs,
            out_specs=sums_spec,
        ),
        **options,
    )(where, near, far, coulomb), near


def term_kernel(where, interp_ref, upper_ref, lower_ref, *refs):
    out_ref = refs[-1]
    piece = jnp.concatenate([upper_ref[...], lower_ref[...]], 0)
    term = lax.dot_general(interp_ref[...], piece, NT, preferred_element_type=jnp.float32)
    out_ref[...] = term if len(refs) == 1 else refs[0][...] + term


def term_of(k, where, interp, upper, lower, total):
    g = interp.shape[0]
    share = upper.shape[1]
    norb = upper.shape[0] + lower.shape[0]
    before = [] if total is None else [total]
    if share % 128:
        block = lax.dynamic_slice_in_dim(interp, where[k] * share, share, 1)
        piece = jnp.concatenate([upper, lower], 0)
        return sum(before, lax.dot_general(block, piece, NT, preferred_element_type=jnp.float32))
    fixed = lambda i, w: (0, 0)
    whole = pl.BlockSpec((g, norb), fixed)
    return pl.pallas_call(
        term_kernel,
        out_shape=jax.ShapeDtypeStruct((g, norb), jnp.float32),
        grid_spec=pltpu.PrefetchScalarGridSpec(
            num_scalar_prefetch=1,
            grid=(1,),
            in_specs=[
                pl.BlockSpec((g, share), lambda i, w: (0, w[k])),
                pl.BlockSpec(upper.shape, fixed),
                pl.BlockSpec(lower.shape, fixed),
            ]
            + [whole] * len(before),
            out_specs=whole,
        ),
        compiler_params=pltpu.CompilerParams(vmem_limit_bytes=16 << 20),
        cost_estimate=pl.CostEstimate(
            flops=2 * g * norb * share, bytes_accessed=2 * g * share, transcendentals=0
        ),
        name="term",
    )(where, pltpu.with_memory_space_constraint(interp, pltpu.HBM), upper, lower, *before)


def local(rows, cols, orbitals, coulomb, interp):
    deal, hop, swap, table = plan(rows, cols)
    share, norb = orbitals.shape
    row, col = lax.axis_index("row"), lax.axis_index("col")
    table = jnp.asarray(table, jnp.int32)
    where = lax.dynamic_slice(table, (row, col, 0), (1, 1, rows + cols)).reshape(rows + cols)

    far = lax.ppermute(orbitals, AXES, deal)
    held = [(0, orbitals)]
    bit = cols // 2
    while bit:
        held += [(mask ^ bit, lax.ppermute(block, AXES, swap(bit))) for mask, block in held]
        bit //= 2
    near = [block for mask, block in sorted(held, key=lambda item: item[0])]

    sent = None
    for k in range(rows):
        following = lax.ppermute(far, AXES, hop) if k < rows - 1 else None
        part, near = partial_of(k, where, near, far, coulomb)
        if sent is not None:
            part = part + lax.ppermute(sent, AXES, hop).astype(jnp.float32)
        sent = part.astype(jnp.bfloat16)
        far = following

    cut = norb // 32 * 16
    upper, lower, total = sent[:cut], sent[cut:], None
    for k in range(rows):
        if total is not None:
            upper, total = lax.optimization_barrier((upper, total))
        if k < rows - 1:
            after = lax.ppermute(upper, AXES, hop), lax.ppermute(lower, AXES, hop)
        total = term_of((k - 1) % rows, where, interp, upper, lower, total)
        upper, lower = after

    bit, blocks = 1, cols
    while bit < cols:
        pairs = total.reshape(blocks // 2, 2, -1, norb)
        mine = (col // bit) % 2
        keep = lax.dynamic_index_in_dim(pairs, mine, 1, keepdims=False)
        give = lax.dynamic_index_in_dim(pairs, 1 - mine, 1, keepdims=False)
        total = keep + lax.ppermute(give.astype(jnp.bfloat16), AXES, swap(bit)).astype(jnp.float32)
        bit, blocks = bit * 2, blocks // 2
    return total.reshape(-1, norb).astype(jnp.bfloat16)


def solution(mesh):
    in_specs = (P(("row", "col"), None), P("row", "col"), P("row", "col"))
    out_specs = P(("row", "col"), None)
    body = functools.partial(local, mesh.shape["row"], mesh.shape["col"])
    return jax.shard_map(body, mesh=mesh, in_specs=in_specs, out_specs=out_specs, check_vma=False)
```

```python
import functools

import jax
import jax.numpy as jnp
from jax import lax
from jax.experimental import pallas as pl
from jax.experimental.pallas import tpu as pltpu
from jax.sharding import PartitionSpec as P


AXES = ("row", "col")
NT = (((1,), (1,)), ((), ()))
TN = (((0,), (0,)), ((), ()))


def plan(rows, cols):
    factor = rows // cols
    half = max(cols // 2, 1)

    def turn(c, target):
        return (c & 1) * half | ((c >> 1) ^ (target & (1 if half > 1 else 0)))

    ring = []
    for y in range(factor):
        zs = range(cols) if y % 2 == 0 else reversed(range(cols))
        ring += [z * factor + y for z in zs]
    position = {row: p for p, row in enumerate(ring)}

    deal, hop, table = [], [], []
    for row in range(rows):
        z, y = divmod(row, factor)
        for c in range(cols):
            deal.append((row * cols + c, (turn(c, z) * factor + y) * cols + z))
    for row in range(rows):
        p = position[row]
        table.append([])
        for c in range(cols):
            back = {turn(s, c): s for s in range(cols)}
            piece = [(r % factor) * cols + back[r // factor] for r in ring]
            step = 1 if c % 2 == 0 else -1
            hop.append((row * cols + c, ring[(p + step) % rows] * cols + c))
            passing = [piece[(p - step * k) % rows] for k in range(rows)]
            table[-1].append(passing + [c ^ mask for mask in range(cols)])

    def swap(bit):
        return [(r * cols + c, r * cols + (c ^ bit)) for r in range(rows) for c in range(cols)]

    return deal, hop, swap, table


def accumulate(near, far_ref, coulomb_ref, out_ref):
    @pl.when(pl.program_id(0) == 0)
    def _():
        out_ref[...] = jnp.zeros_like(out_ref)

    density = lax.dot_general(near, far_ref[...], NT, preferred_element_type=jnp.float32)
    weighted = (coulomb_ref[...] * density).astype(jnp.bfloat16)
    out_ref[...] += lax.dot_general(near, weighted, TN, preferred_element_type=jnp.float32)


def first_kernel(count, where, *refs):
    shards, (far_ref, coulomb_ref, out_ref, near_ref) = refs[:count], refs[count:]
    share = shards[0].shape[0]
    for q in range(count):

        @pl.when(pl.program_id(0) == q)
        def _():
            near_ref[q * share : (q + 1) * share, :] = shards[q][...]

    rows = pl.ds(pl.multiple_of(pl.program_id(0) * share, share), share)
    accumulate(near_ref[rows, :], far_ref, coulomb_ref, out_ref)


def next_kernel(where, near_ref, far_ref, coulomb_ref, out_ref):
    accumulate(near_ref[...], far_ref, coulomb_ref, out_ref)


def partial_of(k, where, near, far, coulomb):
    first = isinstance(near, list)
    count = len(near) if first else near.shape[0] // far.shape[0]
    share, norb = far.shape
    rows = where.shape[0] - count
    if share % 128:
        if first:
            near = jnp.concatenate(near, 0)
        column = lax.dynamic_slice_in_dim(coulomb, where[k] * share, share, 1)
        column = jnp.take(column.reshape(count, share, share), where[rows:], axis=0)
        density = lax.dot_general(near, far, NT, preferred_element_type=jnp.float32)
        weighted = (column.reshape(-1, share) * density).astype(jnp.bfloat16)
        return lax.dot_general(near, weighted, TN, preferred_element_type=jnp.float32), near

    fixed = lambda i, w: (0, 0)
    sums = jax.ShapeDtypeStruct((norb, share), jnp.float32)
    sums_spec = pl.BlockSpec((norb, share), fixed)
    shard_spec = pl.BlockSpec((share, norb), fixed)
    tail_specs = [shard_spec, pl.BlockSpec((share, share), lambda i, w: (w[rows + i], w[k]))]
    m = count * share
    options = dict(
        compiler_params=pltpu.CompilerParams(vmem_limit_bytes=20 << 20),
        cost_estimate=pl.CostEstimate(
            flops=4 * m * norb * share, bytes_accessed=4 * m * share, transcendentals=0
        ),
        name="partial",
    )
    if first:
        return pl.pallas_call(
            functools.partial(first_kernel, count),
            out_shape=(sums, jax.ShapeDtypeStruct((m, norb), jnp.bfloat16)),
            grid_spec=pltpu.PrefetchScalarGridSpec(
                num_scalar_prefetch=1,
                grid=(count,),
                in_specs=[shard_spec] * count + tail_specs,
                out_specs=(sums_spec, pl.BlockSpec((m, norb), fixed)),
            ),
            **options,
        )(where, pltpu.with_memory_space_constraint(near[0], pltpu.HBM), *near[1:], far, coulomb)
    return pl.pallas_call(
        next_kernel,
        out_shape=sums,
        grid_spec=pltpu.PrefetchScalarGridSpec(
            num_scalar_prefetch=1,
            grid=(count,),
            in_specs=[pl.BlockSpec((share, norb), lambda i, w: (i, 0))] + tail_specs,
            out_specs=sums_spec,
        ),
        **options,
    )(where, near, far, coulomb), near


def term_kernel(k, rows, where, interp_ref, upper_ref, lower_ref, *refs):
    refs, sems = list(refs[:-1]), refs[-1]
    share = upper_ref.shape[1]

    def fetch(step, to, sem):
        columns = pl.ds(pl.multiple_of(where[(step - 1) % rows] * share, share), share)
        return pltpu.make_async_copy(interp_ref.at[:, columns], to, sem)

    before = refs.pop(0) if k else None
    block_ref = refs.pop(0) if k else refs.pop()
    out_ref = refs[0]
    copies = [] if k else [fetch(k, block_ref, sems.at[0])]
    if k < rows - 1:
        copies.append(fetch(k + 1, refs[1], sems.at[1]))
    for copy in copies:
        copy.start()
    if not k:
        copies.pop(0).wait()
    piece = jnp.concatenate([upper_ref[...], lower_ref[...]], 0)
    term = lax.dot_general(block_ref[...], piece, NT, preferred_element_type=jnp.float32)
    out_ref[...] = before[...] + term if k else term
    for copy in copies:
        copy.wait()


def term_of(k, rows, where, interp, upper, lower, total, block):
    g = interp.shape[0]
    share = upper.shape[1]
    norb = upper.shape[0] + lower.shape[0]
    last = k == rows - 1
    if share % 128:
        block = lax.dynamic_slice_in_dim(interp, where[(k - 1) % rows] * share, share, 1)
        piece = jnp.concatenate([upper, lower], 0)
        term = lax.dot_general(block, piece, NT, preferred_element_type=jnp.float32)
        return (total + term if k else term), None
    vmem = pl.BlockSpec(memory_space=pltpu.VMEM)
    sums = jax.ShapeDtypeStruct((g, norb), jnp.float32)
    columns = jax.ShapeDtypeStruct((g, share), interp.dtype)
    carried = [total, block] if k else []
    out = pl.pallas_call(
        functools.partial(term_kernel, k, rows),
        out_shape=(sums,) if last else (sums, columns),
        in_specs=[pl.BlockSpec(memory_space=pltpu.SMEM), pl.BlockSpec(memory_space=pltpu.HBM)]
        + [vmem] * (2 + len(carried)),
        out_specs=(vmem,) if last else (vmem, vmem),
        scratch_shapes=([] if k else [pltpu.VMEM(columns.shape, columns.dtype)])
        + [pltpu.SemaphoreType.DMA((2,))],
        compiler_params=pltpu.CompilerParams(vmem_limit_bytes=8 << 20),
        cost_estimate=pl.CostEstimate(
            flops=2 * g * norb * share, bytes_accessed=2 * g * share, transcendentals=0
        ),
        name="term",
    )(where, pltpu.with_memory_space_constraint(interp, pltpu.HBM), upper, lower, *carried)
    return out if len(out) == 2 else (out[0], None)


def local(rows, cols, orbitals, coulomb, interp):
    deal, hop, swap, table = plan(rows, cols)
    _, norb = orbitals.shape
    row, col = lax.axis_index("row"), lax.axis_index("col")
    table = jnp.asarray(table, jnp.int32)
    where = lax.dynamic_slice(table, (row, col, 0), (1, 1, rows + cols)).reshape(rows + cols)

    far = lax.ppermute(orbitals, AXES, deal)
    held = [(0, orbitals)]
    bit = cols // 2
    while bit:
        for mask, block in list(held):
            held.append((mask ^ bit, lax.ppermute(block, AXES, swap(bit))))
        bit //= 2
    near = [block for mask, block in sorted(held, key=lambda item: item[0])]

    sent = None
    for k in range(rows):
        following = lax.ppermute(far, AXES, hop) if k < rows - 1 else None
        part, near = partial_of(k, where, near, far, coulomb)
        if sent is not None:
            part = part + lax.ppermute(sent, AXES, hop).astype(jnp.float32)
        sent = part.astype(jnp.bfloat16)
        far = following

    cut = norb // 32 * 16
    upper, lower, total, block = sent[:cut], sent[cut:], None, None
    for k in range(rows):
        if total is not None:
            upper, total = lax.optimization_barrier((upper, total))
        if k < rows - 1:
            after = lax.ppermute(upper, AXES, hop), lax.ppermute(lower, AXES, hop)
        total, block = term_of(k, rows, where, interp, upper, lower, total, block)
        upper, lower = after

    bit, blocks = 1, cols
    while bit < cols:
        pairs = total.reshape(blocks // 2, 2, -1, norb)
        mine = (col // bit) % 2
        keep = lax.dynamic_index_in_dim(pairs, mine, 1, keepdims=False)
        give = lax.dynamic_index_in_dim(pairs, 1 - mine, 1, keepdims=False)
        total = keep + lax.ppermute(give.astype(jnp.bfloat16), AXES, swap(bit)).astype(jnp.float32)
        bit, blocks = bit * 2, blocks // 2
    return total.reshape(-1, norb).astype(jnp.bfloat16)


def solution(mesh):
    in_specs = (P(("row", "col"), None), P("row", "col"), P("row", "col"))
    out_specs = P(("row", "col"), None)
    rows, cols = mesh.shape["row"], mesh.shape["col"]

    def body(*args):
        return local(rows, cols, *args)

    return jax.shard_map(body, mesh=mesh, in_specs=in_specs, out_specs=out_specs, check_vma=False)
```

```python
import functools

import jax
import jax.numpy as jnp
from jax import lax
from jax.experimental import pallas as pl
from jax.experimental.pallas import tpu as pltpu
from jax.sharding import PartitionSpec as P


AXES = ("row", "col")
NT = (((1,), (1,)), ((), ()))
TN = (((0,), (0,)), ((), ()))


def plan(rows, cols):
    factor = rows // cols
    half = max(cols // 2, 1)

    def turn(c, target):
        return (c & 1) * half | ((c >> 1) ^ (target & (1 if half > 1 else 0)))

    ring = []
    for y in range(factor):
        zs = range(cols) if y % 2 == 0 else reversed(range(cols))
        ring += [z * factor + y for z in zs]
    position = {row: p for p, row in enumerate(ring)}

    deal, hop, table = [], [], []
    for row in range(rows):
        z, y = divmod(row, factor)
        for c in range(cols):
            deal.append((row * cols + c, (turn(c, z) * factor + y) * cols + z))
    for row in range(rows):
        p = position[row]
        table.append([])
        for c in range(cols):
            back = {turn(s, c): s for s in range(cols)}
            piece = [(r % factor) * cols + back[r // factor] for r in ring]
            step = 1 if c % 2 == 0 else -1
            hop.append((row * cols + c, ring[(p + step) % rows] * cols + c))
            passing = [piece[(p - step * k) % rows] for k in range(rows)]
            table[-1].append(passing + [c ^ mask for mask in range(cols)])

    def swap(bit):
        return [(r * cols + c, r * cols + (c ^ bit)) for r in range(rows) for c in range(cols)]

    return deal, hop, swap, table


def accumulate(near, far_ref, coulomb_ref, out_ref):
    @pl.when(pl.program_id(0) == 0)
    def _():
        out_ref[...] = jnp.zeros_like(out_ref)

    density = lax.dot_general(near, far_ref[...], NT, preferred_element_type=jnp.float32)
    weighted = (coulomb_ref[...] * density).astype(jnp.bfloat16)
    out_ref[...] += lax.dot_general(near, weighted, TN, preferred_element_type=jnp.float32)


def first_kernel(count, where, *refs):
    shards, (far_ref, coulomb_ref, out_ref, near_ref) = refs[:count], refs[count:]
    share = shards[0].shape[0]
    start = where[where.shape[0] - count + pl.program_id(0)] * share
    rows = pl.ds(pl.multiple_of(start, share), share)
    for q in range(count):

        @pl.when(pl.program_id(0) == q)
        def _():
            near_ref[rows, :] = shards[q][...]

    accumulate(near_ref[rows, :], far_ref, coulomb_ref, out_ref)


def next_kernel(where, near_ref, far_ref, coulomb_ref, out_ref):
    accumulate(near_ref[...], far_ref, coulomb_ref, out_ref)


def partial_of(k, where, near, far, coulomb):
    first = isinstance(near, list)
    count = len(near) if first else near.shape[0] // far.shape[0]
    share, norb = far.shape
    rows = where.shape[0] - count
    if share % 128:
        if first:
            near = jnp.concatenate(near, 0)
        column = lax.dynamic_slice_in_dim(coulomb, where[k] * share, share, 1)
        column = jnp.take(column.reshape(count, share, share), where[rows:], axis=0)
        density = lax.dot_general(near, far, NT, preferred_element_type=jnp.float32)
        weighted = (column.reshape(-1, share) * density).astype(jnp.bfloat16)
        return lax.dot_general(near, weighted, TN, preferred_element_type=jnp.float32), near

    fixed = lambda i, w: (0, 0)
    sums = jax.ShapeDtypeStruct((norb, share), jnp.float32)
    sums_spec = pl.BlockSpec((norb, share), fixed)
    shard_spec = pl.BlockSpec((share, norb), fixed)
    m = count * share
    tile = 2 * share if count % 2 == 0 else share
    options = dict(
        compiler_params=pltpu.CompilerParams(vmem_limit_bytes=24 << 20),
        cost_estimate=pl.CostEstimate(
            flops=4 * m * norb * share, bytes_accessed=4 * m * share, transcendentals=0
        ),
        name="partial",
    )
    if first:
        return pl.pallas_call(
            functools.partial(first_kernel, count),
            out_shape=(sums, jax.ShapeDtypeStruct((m, norb), jnp.bfloat16)),
            grid_spec=pltpu.PrefetchScalarGridSpec(
                num_scalar_prefetch=1,
                grid=(count,),
                in_specs=[shard_spec] * (count + 1)
                + [pl.BlockSpec((share, share), lambda i, w: (w[rows + i], w[k]))],
                out_specs=(sums_spec, pl.BlockSpec((m, norb), fixed)),
            ),
            **options,
        )(where, pltpu.with_memory_space_constraint(near[0], pltpu.HBM), *near[1:], far, coulomb)
    return pl.pallas_call(
        next_kernel,
        out_shape=sums,
        grid_spec=pltpu.PrefetchScalarGridSpec(
            num_scalar_prefetch=1,
            grid=(m // tile,),
            in_specs=[
                pl.BlockSpec((tile, norb), lambda i, w: (i, 0)),
                shard_spec,
                pl.BlockSpec((tile, share), lambda i, w: (i, w[k])),
            ],
            out_specs=sums_spec,
        ),
        **options,
    )(where, near, far, coulomb), near


def term_kernel(k, rows, where, interp_ref, upper_ref, lower_ref, *refs):
    refs, sems = list(refs[:-1]), refs[-1]
    share = upper_ref.shape[1]

    def fetch(step, to, sem):
        columns = pl.ds(pl.multiple_of(where[(step - 1) % rows] * share, share), share)
        return pltpu.make_async_copy(interp_ref.at[:, columns], to, sem)

    before = refs.pop(0) if k else None
    block_ref = refs.pop(0) if k else refs.pop()
    out_ref = refs[0]
    copies = [] if k else [fetch(k, block_ref, sems.at[0])]
    if k < rows - 1:
        copies.append(fetch(k + 1, refs[1], sems.at[1]))
    for copy in copies:
        copy.start()
    if not k:
        copies.pop(0).wait()
    piece = jnp.concatenate([upper_ref[...], lower_ref[...]], 0)
    term = lax.dot_general(block_ref[...], piece, NT, preferred_element_type=jnp.float32)
    out_ref[...] = before[...] + term if k else term
    for copy in copies:
        copy.wait()


def term_of(k, rows, where, interp, upper, lower, total, block):
    g = interp.shape[0]
    share = upper.shape[1]
    norb = upper.shape[0] + lower.shape[0]
    last = k == rows - 1
    if share % 128:
        block = lax.dynamic_slice_in_dim(interp, where[(k - 1) % rows] * share, share, 1)
        piece = jnp.concatenate([upper, lower], 0)
        term = lax.dot_general(block, piece, NT, preferred_element_type=jnp.float32)
        return (total + term if k else term), None
    vmem = pl.BlockSpec(memory_space=pltpu.VMEM)
    sums = jax.ShapeDtypeStruct((g, norb), jnp.float32)
    columns = jax.ShapeDtypeStruct((g, share), interp.dtype)
    carried = [total, block] if k else []
    out = pl.pallas_call(
        functools.partial(term_kernel, k, rows),
        out_shape=(sums,) if last else (sums, columns),
        in_specs=[pl.BlockSpec(memory_space=pltpu.SMEM), pl.BlockSpec(memory_space=pltpu.HBM)]
        + [vmem] * (2 + len(carried)),
        out_specs=(vmem,) if last else (vmem, vmem),
        scratch_shapes=([] if k else [pltpu.VMEM(columns.shape, columns.dtype)])
        + [pltpu.SemaphoreType.DMA((2,))],
        compiler_params=pltpu.CompilerParams(vmem_limit_bytes=8 << 20),
        cost_estimate=pl.CostEstimate(
            flops=2 * g * norb * share, bytes_accessed=2 * g * share, transcendentals=0
        ),
        name="term",
    )(where, pltpu.with_memory_space_constraint(interp, pltpu.HBM), upper, lower, *carried)
    return out if len(out) == 2 else (out[0], None)


def local(rows, cols, orbitals, coulomb, interp):
    deal, hop, swap, table = plan(rows, cols)
    _, norb = orbitals.shape
    row, col = lax.axis_index("row"), lax.axis_index("col")
    far = lax.ppermute(orbitals, AXES, deal)
    far, landed = lax.optimization_barrier((far, row))
    table = jnp.asarray(table, jnp.int32)
    where = lax.dynamic_slice(table, (landed, col, 0), (1, 1, rows + cols)).reshape(-1)

    held = [(0, orbitals)]
    bit = cols // 2
    while bit:
        for mask, block in list(held):
            held.append((mask ^ bit, lax.ppermute(block, AXES, swap(bit))))
        bit //= 2
    near = [block for mask, block in sorted(held, key=lambda item: item[0])]

    sent = None
    for k in range(rows):
        following = lax.ppermute(far, AXES, hop) if k < rows - 1 else None
        part, near = partial_of(k, where, near, far, coulomb)
        if sent is not None:
            part = part + lax.ppermute(sent, AXES, hop).astype(jnp.float32)
        sent = part.astype(jnp.bfloat16)
        far = following

    cut = norb // 32 * 16
    upper, lower, total, block = sent[:cut], sent[cut:], None, None
    for k in range(rows):
        if k < rows - 1:
            upper_next = lax.ppermute(upper, AXES, hop)
            lower_next = lax.ppermute(lower, AXES, hop)
        total, block = term_of(k, rows, where, interp, upper, lower, total, block)
        upper, lower = upper_next, lower_next

    bit, blocks = 1, cols
    while bit < cols:
        pairs = total.reshape(blocks // 2, 2, -1, norb)
        mine = (col // bit) % 2
        keep = lax.dynamic_index_in_dim(pairs, mine, 1, keepdims=False)
        give = lax.dynamic_index_in_dim(pairs, 1 - mine, 1, keepdims=False)
        total = keep + lax.ppermute(give.astype(jnp.bfloat16), AXES, swap(bit)).astype(jnp.float32)
        bit, blocks = bit * 2, blocks // 2
    return total.reshape(-1, norb).astype(jnp.bfloat16)


def solution(mesh):
    in_specs = (P(("row", "col"), None), P("row", "col"), P("row", "col"))
    out_specs = P(("row", "col"), None)
    rows, cols = mesh.shape["row"], mesh.shape["col"]

    def body(*args):
        return local(rows, cols, *args)

    return jax.shard_map(body, mesh=mesh, in_specs=in_specs, out_specs=out_specs, check_vma=False)
```
